32 devices in a mesh: dp: 4 (over y, x), tensor: 8 (over z, core).
Axes of the slice: x: 2, y: 2, z: 4, core: 2. Of those that a mesh axis runs over, the one named last changes fastest.
Arguments:
- tokens: bfloat16 [96, 8192], P(('dp', 'tensor')), may hold values from -6 to 6
- weight_store: bfloat16 [2, 192, 128, 128], P(None, 'tensor', 'dp'), may hold values from -0.25 to 0.25
- block_cols: int32 [24, 8], P('tensor'), may hold values from 0 to 63, as said below
- block_count: int32 [24], P('tensor'), may hold values from 1 to 8, 108 in all
- block_home: int32 [8, 24], P('tensor'), may hold values from 0 to 23, each once within a row
- grad_hidden: bfloat16 [96, 3072], P('dp', 'tensor'), may hold values from -6 to 6
Outputs:
- hidden: bfloat16 [96, 3072], P('dp', 'tensor')
- grad_tokens: bfloat16 [96, 8192], P(('dp', 'tensor'))
- grad_weights: bfloat16 [2, 192, 128, 128], P(None, 'tensor', 'dp')
The draws below stay inside these ranges and needn't reach their ends.
Inputs may be any that keep to these rules, and one draw needn't show every extreme that they name: `block_cols`: the 8 column blocks listed for one hidden block are all different. `block_count`: some hidden block has all 8 slots present. `block_home`: each row is a permutation of 0 to 23.
All inputs are finite; a program needn't handle non-finite values.
Results may differ from the reference program's by a relative error of at most 0.009.
Values may be sent and summed in bfloat16 or wider, within the bound.
A program may use at most 64 MiB of HBM per device.

```python
import math
import jax
import jax.numpy as jnp
import numpy as np
from jax import lax

D = 8192
BLK = 128
KMAX = 8
HB_DEV = 3
HB = 24
FF = 3072
DBLK = 64
SLOTS = 24
NS = 192
GROUP_ROWS = 24
TOKENS = 96
N_DP = 4
N_TENSOR = 8


def draw_block_cols(key, part):
    keys = jax.random.split(key, HB)
    picked = jax.vmap(lambda one_key: jax.random.permutation(one_key, DBLK)[:KMAX])(keys)
    return picked.astype(jnp.int32)


def steps_of(own_key, dims, pieces, low, largest):
    gain, own = 1.0, jax.random.fold_in(own_key, 6)
    for position, shards_of in pieces:
        draws = jnp.exp(jax.random.uniform(jax.random.fold_in(own, position), (shards_of,), jnp.float32, low / len(pieces), largest / len(pieces)))
        gain = gain * jnp.repeat(draws, dims[position] // shards_of).reshape([-1 if axis == position else 1 for axis in range(len(dims))])
    return gain


def split_up(amount, total, most, slope):
    weights = [(1 << 20) // math.isqrt(standing ** slope) + 1 for standing in range(2, amount + 1)]
    rest, counts = total - most - (amount - 1), [1] * (amount - 1)
    while rest > 0:
        candidates = [i for i in range(amount - 1) if counts[i] < most]
        mass, remaining = sum([weights[i] for i in candidates]), rest
        for i in candidates:
            extra = min(most - counts[i], max(1, remaining * weights[i] // mass), rest)
            counts[i] = counts[i] + extra
            rest = rest - extra
    return np.array([most] + counts)


def uneven_parts(stream_key, count, total, bound, slope):
    if count == 2:
        one = jax.random.randint(stream_key, (), max(1, total - bound), min(bound, total - 1) + 1)
        return jnp.stack([one, total - one])
    tallies = jnp.asarray(split_up(count, total, bound, slope), jnp.int32)
    twos = (count - 1) // 2
    source_of, taker = tallies[1:1 + 2 * twos:2], tallies[2:2 + 2 * twos:2]
    slack = jnp.minimum(source_of - 1, bound - taker)
    moved = jax.random.randint(jax.random.fold_in(stream_key, 1), (twos,), 0, 1 << 20) % (slack + 1)
    tallies = tallies.at[1:1 + 2 * twos:2].set(source_of - moved).at[2:2 + 2 * twos:2].set(taker + moved)
    return tallies[jax.random.permutation(jax.random.fold_in(stream_key, 2), count)]


def scatter_about(rng, extent, width, most, shards=(), held_as=jnp.bfloat16):
    level = steps_of(rng, extent, shards, -0.22, 0.18) if shards else 1.0
    entries = jax.random.normal(rng, extent, jnp.float32) * width * level
    return jnp.minimum(jnp.maximum(entries, -most), most).astype(held_as)


def setup_inputs(seed: int = 0) -> dict:
    splits = jax.random.split(jax.random.key(seed), 7)
    tokens = scatter_about(splits[0], (TOKENS, D), 1.0, 6.0, ((0, 32),))
    weight_store = scatter_about(splits[1], (2, NS, BLK, BLK), (KMAX * BLK // 2) ** -0.5, 0.25, ((1, 8), (2, 4)))
    block_cols = draw_block_cols(jax.random.fold_in(splits[6], 71), 0)
    block_count = uneven_parts(splits[3], HB, HB * (KMAX + 1) // 2, KMAX, 2).astype(jnp.int32)
    block_home = jax.vmap(lambda own: jax.random.permutation(own, SLOTS))(jax.random.split(splits[4], N_TENSOR)).reshape((N_TENSOR, SLOTS)).astype(jnp.int32)
    grad_hidden = scatter_about(splits[5], (TOKENS, FF), 1.0, 6.0, ((0, 4), (1, 8)))
    return {"tokens": tokens, "weight_store": weight_store, "block_cols": block_cols, "block_count": block_count, "block_home": block_home, "grad_hidden": grad_hidden}


def round_bf16(value):
    return lax.optimization_barrier(value.astype(jnp.bfloat16)).astype(jnp.float32)


def reference(tokens, weight_store, block_cols, block_count, block_home, grad_hidden):
    owner_group = jnp.arange(HB, dtype=jnp.int32) // HB_DEV
    local_slot = (jnp.arange(HB, dtype=jnp.int32) % HB_DEV)[:, None] * KMAX + jnp.arange(KMAX, dtype=jnp.int32)[None, :]
    home_slots = block_home[owner_group[:, None], local_slot]
    positions = (owner_group[:, None] * SLOTS + home_slots).astype(jnp.int32)
    present = (jnp.arange(KMAX, dtype=jnp.int32)[None, :] < block_count[:, None]).astype(jnp.bfloat16)
    token_blocks = tokens.reshape(TOKENS, DBLK, BLK)
    grad_cols = grad_hidden.reshape(TOKENS, HB, BLK).transpose(1, 0, 2)

    def slot_step(running, per_block):
        columns, rows_pos, mask_row, grad_in = per_block
        block_weights = weight_store[:, rows_pos] * mask_row[None, :, None, None]
        float_weights = block_weights.astype(jnp.float32)
        picked = jnp.take(token_blocks, columns, axis=1).astype(jnp.float32)
        gate_pre = jnp.einsum('tkb,kbc->tc', picked, float_weights[0])
        up_pre = jnp.einsum('tkb,kbc->tc', picked, float_weights[1])
        gate_sigma = jax.nn.sigmoid(gate_pre)
        activated = gate_pre * gate_sigma
        hidden_block = (activated * up_pre).astype(jnp.bfloat16)
        grad_f = grad_in.astype(jnp.float32)
        grad_gate = round_bf16(grad_f * up_pre * gate_sigma * (1.0 + gate_pre * (1.0 - gate_sigma)))
        grad_up = round_bf16(grad_f * activated)
        back_term = jnp.einsum('tc,kbc->tkb', grad_gate, float_weights[0]) + jnp.einsum('tc,kbc->tkb', grad_up, float_weights[1])
        running = running.at[:, columns].add(back_term)
        grouped = picked.reshape(N_DP, GROUP_ROWS, KMAX, BLK)
        part_gate = jnp.einsum('ntkb,ntc->nkbc', grouped, grad_gate.reshape(N_DP, GROUP_ROWS, BLK))
        part_up = jnp.einsum('ntkb,ntc->nkbc', grouped, grad_up.reshape(N_DP, GROUP_ROWS, BLK))
        grad_blocks = jnp.stack([part_gate, part_up])
        grad_blocks = round_bf16(grad_blocks).sum(axis=1) * mask_row.astype(jnp.float32)[None, :, None, None]
        return running, (hidden_block, grad_blocks)

    start_grads = jnp.zeros((TOKENS, DBLK, BLK), jnp.float32)
    token_grads, (hidden_all, grad_all) = lax.scan(slot_step, start_grads, (block_cols, positions, present, grad_cols))
    hidden = hidden_all.transpose(1, 0, 2).reshape(TOKENS, FF)
    flat_grads = grad_all.transpose(1, 0, 2, 3, 4).reshape(2, HB * KMAX, BLK, BLK)
    grad_weights = jnp.zeros((2, NS, BLK, BLK), jnp.float32).at[:, positions.reshape(-1)].set(flat_grads)
    return hidden, token_grads.reshape(TOKENS, D).astype(jnp.bfloat16), grad_weights.astype(jnp.bfloat16)
```

```python
import functools
import jax
import jax.numpy as jnp
from jax import lax
from jax.experimental import pallas as pl
from jax.experimental.pallas import tpu as pltpu
from jax.sharding import PartitionSpec as P

MESH = pl.DeviceIdType.MESH
F32 = jnp.float32
BF16 = jnp.bfloat16
LANES = 128


def exchange_kernel(
    n_dp, n_t, cols_s, count_s, home_s, cols_v, tok_ref, w_ref, gh_ref,
    hid_ref, wg_ref, cr_ref, ca_ref,
    tq, x, xt, wb, ps, pr, ga, cf, c,
    s1, r1, s2, r2, sc, rc, sp, rp, sg, rg, st, rt, loc,
):
    n_dev = n_dp * n_t
    me_n, me_t = lax.axis_index("dp"), lax.axis_index("tensor")
    me = me_n * n_t + me_t
    own, blocks, _ = tok_ref.shape
    rows = w_ref.shape[2]
    blk = w_ref.shape[3]
    hb, kmax = cols_s.shape
    groups = LANES // rows
    tiles = blocks // groups
    tokens = own * n_dev
    group_rows = own * n_t
    span = kmax * rows

    barrier = pltpu.get_barrier_semaphore()

    def greet(i, carry):
        o = lax.rem(me + i, n_dev)
        pl.semaphore_signal(barrier, inc=1, device_id=(o // n_t, lax.rem(o, n_t)), device_id_type=MESH)
        return carry

    lax.fori_loop(1, n_dev, greet, 0)

    tok = tok_ref[...].astype(F32)
    for n in range(n_dp):
        tq[n] = jnp.concatenate(
            [tok[:, g * tiles:(g + 1) * tiles, n * rows:(n + 1) * rows] for g in range(groups)], axis=2
        ).astype(BF16)
    for h in range(hb):
        for m in range(2):
            parts = []
            for k in range(kmax):
                keep = jnp.where(k < count_s[h], 1.0, 0.0).astype(F32)
                parts.append(w_ref[m, home_s[0, h * kmax + k]].astype(F32) * keep)
            wb[h, :, m * blk:(m + 1) * blk] = jnp.concatenate(parts, axis=0).astype(BF16)
    pl.semaphore_wait(barrier, n_dev - 1)

    own_tok = pltpu.make_async_copy(tq.at[me_n], x.at[me_n, me_t], loc.at[0])
    own_tok.start()
    own_cols = pltpu.make_async_copy(cols_v, ca_ref.at[me_t], loc.at[1])
    own_cols.start()

    def first(d):
        n = lax.rem(me_n + d, n_dp)
        return pltpu.make_async_remote_copy(
            src_ref=tq.at[n], dst_ref=x.at[me_n, me_t], send_sem=s1.at[d], recv_sem=r1.at[d],
            device_id=(n, me_t), device_id_type=MESH)

    def second(e):
        t = lax.rem(me_t + e, n_t)
        return pltpu.make_async_remote_copy(
            src_ref=x.at[:, me_t], dst_ref=x.at[:, me_t], send_sem=s2.at[e], recv_sem=r2.at[e],
            device_id=(me_n, t), device_id_type=MESH)

    def columns(e):
        t = lax.rem(me_t + e, n_t)
        return pltpu.make_async_remote_copy(
            src_ref=cols_v, dst_ref=ca_ref.at[me_t], send_sem=sc.at[e], recv_sem=rc.at[e],
            device_id=(me_n, t), device_id_type=MESH)

    def partial(d):
        n = lax.rem(me_n + d, n_dp)
        return pltpu.make_async_remote_copy(
            src_ref=ps.at[n], dst_ref=pr.at[d], send_sem=sp.at[d], recv_sem=rp.at[d],
            device_id=(n, me_t), device_id_type=MESH)

    def grads(d):
        n = lax.rem(me_n + d, n_dp)
        return pltpu.make_async_remote_copy(
            src_ref=ga.at[me_n], dst_ref=ga.at[me_n], send_sem=sg.at[d], recv_sem=rg.at[d],
            device_id=(n, me_t), device_id_type=MESH)

    def terms(i):
        o = lax.rem(me + i, n_dev)
        n, t = o // n_t, lax.rem(o, n_t)
        return pltpu.make_async_remote_copy(
            src_ref=c.at[n, t], dst_ref=cr_ref.at[me_n, me_t], send_sem=st.at[i], recv_sem=rt.at[i],
            device_id=(n, t), device_id_type=MESH)

    def each(count, act):
        lax.fori_loop(1, count, lambda i, carry: (act(i), carry)[1], 0)

    each(n_dp, lambda d: first(d).start())
    each(n_t, lambda e: columns(e).start())
    own_tok.wait()
    each(n_dp, lambda d: first(d).wait_recv())
    each(n_t, lambda e: second(e).start())
    each(n_t, lambda e: second(e).wait_recv())

    flat = x[...].reshape(tokens, tiles, LANES).astype(F32)
    turned = jnp.swapaxes(flat, 0, 1)
    for j in range(tiles):
        upright = turned[j].T
        for g in range(groups):
            xt[g * tiles + j] = upright[g * rows:(g + 1) * rows]

    picked, mine = [], []
    for h in range(hb):
        chosen = jnp.concatenate([xt[cols_s[h, k]] for k in range(kmax)], axis=0).astype(BF16)
        picked.append(chosen)
        pre = lax.dot_general(chosen, wb[h], (((0,), (0,)), ((), ())), preferred_element_type=F32)
        for n in range(n_dp):
            ps[n, :, h * 2 * blk:(h + 1) * 2 * blk] = pre[n * group_rows:(n + 1) * group_rows].astype(BF16)
    each(n_dp, lambda d: partial(d).start())
    total = ps[me_n].astype(F32)
    each(n_dp, lambda d: partial(d).wait_recv())
    for d in range(1, n_dp):
        total = total + pr[d].astype(F32)
    grad_parts = []
    for h in range(hb):
        gate = total[:, h * 2 * blk:(h * 2 + 1) * blk]
        up = total[:, (h * 2 + 1) * blk:(h + 1) * 2 * blk]
        grad_in = gh_ref[:, h * blk:(h + 1) * blk].astype(F32)
        sigma = jax.nn.sigmoid(gate)
        act = gate * sigma
        hid_ref[:, h * blk:(h + 1) * blk] = (act * up).astype(BF16)
        grad_parts += [grad_in * up * sigma * (1.0 + gate * (1.0 - sigma)), grad_in * act]
    ga[me_n] = jnp.concatenate(grad_parts, axis=1).astype(BF16)
    each(n_dp, lambda d: grads(d).start())
    each(n_dp, lambda d: grads(d).wait_recv())

    every = jnp.concatenate([ga[n].astype(F32) for n in range(n_dp)], axis=0).astype(BF16)
    for h in range(hb):
        cf[:, h * span:(h + 1) * span] = lax.dot_general(
            every[:, h * 2 * blk:(h + 1) * 2 * blk], wb[h], (((1,), (1,)), ((), ())), preferred_element_type=F32)
    for n in range(n_dp):
        part = cf[n * group_rows:(n + 1) * group_rows, :]
        for t in range(n_t):
            c[n, t] = part[t * own:(t + 1) * own].astype(BF16)
    own_terms = pltpu.make_async_copy(c.at[me_n, me_t], cr_ref.at[me_n, me_t], loc.at[2])
    own_terms.start()
    each(n_dev, lambda i: terms(i).start())

    for h in range(hb):
        grown = jnp.dot(picked[h], every[:, h * 2 * blk:(h + 1) * 2 * blk], preferred_element_type=F32)
        for k in range(kmax):
            keep = jnp.where(k < count_s[h], 1.0, 0.0).astype(F32)
            for m in range(2):
                wg_ref[m, h * kmax + k] = (
                    grown[k * rows:(k + 1) * rows, m * blk:(m + 1) * blk] * keep).astype(BF16)

    own_cols.wait()
    own_terms.wait()
    each(n_dev, lambda i: terms(i).wait_recv())
    each(n_t, lambda e: columns(e).wait_recv())
    each(n_dp, lambda d: first(d).wait_send())
    each(n_t, lambda e: second(e).wait_send())
    each(n_t, lambda e: columns(e).wait_send())
    each(n_dp, lambda d: partial(d).wait_send())
    each(n_dp, lambda d: grads(d).wait_send())
    each(n_dev, lambda i: terms(i).wait_send())


def place_kernel(cr_ref, ca_s, home_s, hid_in, wg_in, hid_ref, gt_ref, gw_ref, acc):
    n_dp, n_t, own, _ = cr_ref.shape
    rows, blk = wg_in.shape[2:]
    slots = wg_in.shape[1]
    kmax = ca_s.shape[2]
    blocks = acc.shape[0]
    hid_ref[...] = hid_in[...]
    for s in range(slots):
        spot = home_s[0, s]
        for m in range(2):
            gw_ref[m, spot] = wg_in[m, s]
    acc[...] = jnp.zeros_like(acc)

    def group(t, carry):
        sources = [cr_ref[n, t].astype(F32) for n in range(n_dp)]
        for s in range(slots):
            col = ca_s[t, s // kmax, s % kmax]
            acc[col] += jnp.concatenate([v[:, s * rows:(s + 1) * rows] for v in sources], axis=1)
        return carry

    lax.fori_loop(0, n_t, group, 0)
    for b in range(blocks):
        gt_ref[:, b * blk:(b + 1) * blk] = acc[b].astype(BF16)


def body(n_dp, n_t, tokens, weight_store, block_cols, block_count, block_home, grad_hidden):
    own, width = tokens.shape
    _, slots, rows, blk = weight_store.shape
    blocks = width // blk
    hb, kmax = block_cols.shape
    n_dev = n_dp * n_t
    group_rows = own * n_t
    groups = LANES // rows
    tiles = blocks // groups
    ff = hb * blk
    vmem = pl.BlockSpec(memory_space=pltpu.VMEM)
    smem = pl.BlockSpec(memory_space=pltpu.SMEM)
    dma = pltpu.SemaphoreType.DMA
    hid, wg, cr, ca = pl.pallas_call(
        functools.partial(exchange_kernel, n_dp, n_t),
        out_shape=(
            jax.ShapeDtypeStruct((group_rows, ff), BF16),
            jax.ShapeDtypeStruct((2, slots, rows, blk), BF16),
            jax.ShapeDtypeStruct((n_dp, n_t, own, slots * rows), BF16),
            jax.ShapeDtypeStruct((n_t, hb, kmax), jnp.int32),
        ),
        in_specs=[smem, smem, smem, vmem, vmem, vmem, vmem],
        out_specs=(vmem, vmem, vmem, vmem),
        scratch_shapes=[
            pltpu.VMEM((n_dp, own, tiles, LANES), BF16),
            pltpu.VMEM((n_dp, n_t, own, tiles, LANES), BF16),
            pltpu.VMEM((blocks, rows, own * n_dev), F32),
            pltpu.VMEM((hb, kmax * rows, 2 * blk), BF16),
            pltpu.VMEM((n_dp, group_rows, 2 * ff), BF16),
            pltpu.VMEM((n_dp, group_rows, 2 * ff), BF16),
            pltpu.VMEM((n_dp, group_rows, 2 * ff), BF16),
            pltpu.VMEM((own * n_dev, slots * rows), F32),
            pltpu.VMEM((n_dp, n_t, own, slots * rows), BF16),
            dma((n_dp,)), dma((n_dp,)), dma((n_t,)), dma((n_t,)), dma((n_t,)), dma((n_t,)),
            dma((n_dp,)), dma((n_dp,)), dma((n_dp,)), dma((n_dp,)), dma((n_dev,)), dma((n_dev,)),
            dma((3,)),
        ],
        compiler_params=pltpu.CompilerParams(
            collective_id=0, has_side_effects=True, vmem_limit_bytes=56 * 1024 * 1024),
        name="exchange",
    )(block_cols, block_count, block_home, block_cols, tokens.reshape(own, blocks, blk), weight_store, grad_hidden)
    return pl.pallas_call(
        place_kernel,
        out_shape=(
            jax.ShapeDtypeStruct((group_rows, ff), BF16),
            jax.ShapeDtypeStruct((own, width), BF16),
            jax.ShapeDtypeStruct((2, slots, rows, blk), BF16),
        ),
        in_specs=[vmem, smem, smem, vmem, vmem],
        out_specs=(vmem, vmem, vmem),
        scratch_shapes=[pltpu.VMEM((blocks, own, LANES), F32)],
        compiler_params=pltpu.CompilerParams(vmem_limit_bytes=32 * 1024 * 1024),
        name="place",
    )(cr, ca, block_home, hid, wg)


def solution(mesh):
    return jax.shard_map(
        functools.partial(body, mesh.shape["dp"], mesh.shape["tensor"]),
        mesh=mesh,
        in_specs=(
            P(("dp", "tensor"), None),
            P(None, "tensor", "dp", None),
            P("tensor", None),
            P("tensor"),
            P("tensor", None),
            P("dp", "tensor"),
        ),
        out_specs=(P("dp", "tensor"), P(("dp", "tensor"), None), P(None, "tensor", "dp", None)),
        check_vma=False,
    )
```

```python
import functools
import jax
import jax.numpy as jnp
from jax import lax
from jax.experimental import pallas as pl
from jax.experimental.pallas import tpu as pltpu
from jax.sharding import PartitionSpec as P

MESH = pl.DeviceIdType.MESH
F32 = jnp.float32
BF16 = jnp.bfloat16
LANES = 128


def exchange_kernel(
    n_dp, n_t, cols_s, count_s, home_s, cols_v, tok_ref, w_hbm, gh_ref,
    hid_out, wg_out, cr_ref, ca_ref,
    wv, tq, x, xt, wb, ps, pr, ga, c, hid_ref, wg_ref,
    s1, r1, s2, r2, sc, rc, sp, rp, sg, rg, st, rt, loc,
):
    n_dev = n_dp * n_t
    me_n, me_t = lax.axis_index("dp"), lax.axis_index("tensor")
    me = me_n * n_t + me_t
    own, width = tok_ref.shape
    rows = w_hbm.shape[2]
    blk = w_hbm.shape[3]
    blocks = width // blk
    hb, kmax = cols_s.shape
    groups = LANES // rows
    tiles = blocks // groups
    tokens = own * n_dev
    group_rows = own * n_t
    span = kmax * rows

    barrier = pltpu.get_barrier_semaphore()

    def greet(i, carry):
        o = lax.rem(me + i, n_dev)
        pl.semaphore_signal(barrier, inc=1, device_id=(o // n_t, lax.rem(o, n_t)), device_id_type=MESH)
        return carry

    lax.fori_loop(1, n_dev, greet, 0)
    fetch = pltpu.make_async_copy(w_hbm, wv, loc.at[0])
    fetch.start()

    flat_tok = tok_ref[...].astype(F32)
    tok = jnp.stack([flat_tok[:, b * blk:(b + 1) * blk] for b in range(blocks)], axis=1)
    for n in range(n_dp):
        tq[n] = jnp.concatenate(
            [tok[:, g * tiles:(g + 1) * tiles, n * rows:(n + 1) * rows] for g in range(groups)], axis=2
        ).astype(BF16)
    fetch.wait()
    for h in range(hb):
        for m in range(2):
            parts = []
            for k in range(kmax):
                keep = jnp.where(k < count_s[h], 1.0, 0.0).astype(F32)
                parts.append(wv[m, home_s[0, h * kmax + k]].astype(F32) * keep)
            wb[h, :, m * blk:(m + 1) * blk] = jnp.concatenate(parts, axis=0).astype(BF16)
    pl.semaphore_wait(barrier, n_dev - 1)

    def ahead(d):
        return lax.rem(me_n + d, n_dp)

    def behind(d):
        return lax.rem(me_n - d + n_dp, n_dp)

    def first(d):
        n = ahead(d)
        return pltpu.make_async_remote_copy(
            src_ref=tq.at[n], dst_ref=x.at[me_n, me_t], send_sem=s1.at[d], recv_sem=r1.at[d],
            device_id=(n, me_t), device_id_type=MESH)

    def second(d, e):
        n, t = behind(d), lax.rem(me_t + e, n_t)
        return pltpu.make_async_remote_copy(
            src_ref=x.at[n, me_t], dst_ref=x.at[n, me_t], send_sem=s2.at[d, e], recv_sem=r2.at[d, e],
            device_id=(me_n, t), device_id_type=MESH)

    def columns(e):
        t = lax.rem(me_t + e, n_t)
        return pltpu.make_async_remote_copy(
            src_ref=cols_v, dst_ref=ca_ref.at[me_t], send_sem=sc.at[e], recv_sem=rc.at[e],
            device_id=(me_n, t), device_id_type=MESH)

    def partial(h, d):
        n = ahead(d)
        return pltpu.make_async_remote_copy(
            src_ref=ps.at[h, n], dst_ref=pr.at[h, d], send_sem=sp.at[h, d], recv_sem=rp.at[h, d],
            device_id=(n, me_t), device_id_type=MESH)

    def grads(h, d):
        n = ahead(d)
        return pltpu.make_async_remote_copy(
            src_ref=ga.at[h, me_n], dst_ref=ga.at[h, me_n], send_sem=sg.at[h, d], recv_sem=rg.at[h, d],
            device_id=(n, me_t), device_id_type=MESH)

    def terms(d, e):
        n, t = behind(d), lax.rem(me_t + e, n_t)
        return pltpu.make_async_remote_copy(
            src_ref=c.at[n, t], dst_ref=cr_ref.at[me_n, me_t], send_sem=st.at[d, e], recv_sem=rt.at[d, e],
            device_id=(n, t), device_id_type=MESH)

    def each(count, act, start=1):
        lax.fori_loop(start, count, lambda i, carry: (act(i), carry)[1], 0)

    each(n_dp, lambda d: first(d).start())
    own_tok = pltpu.make_async_copy(tq.at[me_n], x.at[me_n, me_t], loc.at[0])
    own_tok.start()
    own_cols = pltpu.make_async_copy(cols_v, ca_ref.at[me_t], loc.at[1])
    own_cols.start()
    own_tok.wait()
    each(n_t, lambda e: second(0, e).start())

    def relay(d):
        first(d).wait_recv()
        each(n_t, lambda e: second(d, e).start())

    each(n_dp, relay)
    each(n_t, lambda e: columns(e).start())
    each(n_dp, lambda d: each(n_t, lambda e: second(d, e).wait_recv()), 0)

    flat = x[...].reshape(tokens, tiles, LANES).astype(F32)
    turned = jnp.swapaxes(flat, 0, 1)
    for j in range(tiles):
        upright = turned[j].T
        for g in range(groups):
            xt[g * tiles + j] = upright[g * rows:(g + 1) * rows]

    picked = []
    for h in range(hb):
        chosen = jnp.concatenate([xt[cols_s[h, k]] for k in range(kmax)], axis=0).astype(BF16)
        picked.append(chosen)
        pre = lax.dot_general(chosen, wb[h], (((0,), (0,)), ((), ())), preferred_element_type=F32)
        for n in range(n_dp):
            ps[h, n] = pre[n * group_rows:(n + 1) * group_rows].astype(BF16)
        each(n_dp, lambda d: partial(h, d).start())
    for h in range(hb):
        total = ps[h, me_n].astype(F32)
        each(n_dp, lambda d: partial(h, d).wait_recv())
        for d in range(1, n_dp):
            total = total + pr[h, d].astype(F32)
        gate, up = total[:, :blk], total[:, blk:]
        grad_in = gh_ref[:, h * blk:(h + 1) * blk].astype(F32)
        sigma = jax.nn.sigmoid(gate)
        act = gate * sigma
        hid_ref[:, h * blk:(h + 1) * blk] = (act * up).astype(BF16)
        ga[h, me_n] = jnp.concatenate(
            [grad_in * up * sigma * (1.0 + gate * (1.0 - sigma)), grad_in * act], axis=1).astype(BF16)
        each(n_dp, lambda d: grads(h, d).start())
    hid_copy = pltpu.make_async_copy(hid_ref, hid_out, loc.at[0])
    hid_copy.start()

    def send_terms(n):
        part = jnp.concatenate([
            lax.dot_general(ga[h, n], wb[h], (((1,), (1,)), ((), ())), preferred_element_type=F32)
            for h in range(hb)], axis=1)
        for t in range(n_t):
            c[n, t] = part[t * own:(t + 1) * own].astype(BF16)

    send_terms(me_n)
    own_terms = pltpu.make_async_copy(c.at[me_n, me_t], cr_ref.at[me_n, me_t], loc.at[2])
    own_terms.start()
    each(n_t, lambda e: terms(0, e).start())

    def others(d):
        for h in range(hb):
            grads(h, d).wait_recv()
        send_terms(behind(d))
        each(n_t, lambda e: terms(d, e).start(), 0)

    each(n_dp, others)

    for h in range(hb):
        every = jnp.concatenate([ga[h, n].astype(F32) for n in range(n_dp)], axis=0).astype(BF16)
        grown = jnp.dot(picked[h], every, preferred_element_type=F32)
        for k in range(kmax):
            keep = jnp.where(k < count_s[h], 1.0, 0.0).astype(F32)
            for m in range(2):
                wg_ref[m, h * kmax + k] = (
                    grown[k * rows:(k + 1) * rows, m * blk:(m + 1) * blk] * keep).astype(BF16)
    wg_copy = pltpu.make_async_copy(wg_ref, wg_out, loc.at[3])
    wg_copy.start()

    own_cols.wait()
    own_terms.wait()
    hid_copy.wait()
    each(n_t, lambda e: terms(0, e).wait_recv())
    each(n_dp, lambda d: each(n_t, lambda e: terms(d, e).wait_recv(), 0))
    each(n_t, lambda e: columns(e).wait_recv())
    each(n_dp, lambda d: first(d).wait_send())
    each(n_dp, lambda d: each(n_t, lambda e: second(d, e).wait_send()), 0)
    each(n_t, lambda e: columns(e).wait_send())
    for h in range(hb):
        each(n_dp, lambda d: partial(h, d).wait_send())
        each(n_dp, lambda d: grads(h, d).wait_send())
    each(n_t, lambda e: terms(0, e).wait_send())
    each(n_dp, lambda d: each(n_t, lambda e: terms(d, e).wait_send(), 0))
    wg_copy.wait()


def place_kernel(cr_ref, ca_s, home_s, hid_in, wg_in, hid_ref, gt_ref, gw_out, acc, wv, fetched, sent):
    n_dp, n_t, own, _ = cr_ref.shape
    rows, blk = wg_in.shape[2:]
    slots = wg_in.shape[1]
    kmax = ca_s.shape[2]
    blocks = acc.shape[0]

    def fetch(s):
        return pltpu.make_async_copy(wg_in.at[:, s], wv.at[:, home_s[0, s]], fetched.at[s])

    for s in range(slots):
        fetch(s).start()
    hid_ref[...] = hid_in[...]
    acc[...] = jnp.zeros_like(acc)
    for s in range(slots):
        fetch(s).wait()
    put = pltpu.make_async_copy(wv, gw_out, sent)
    put.start()

    def group(t, carry):
        sources = [cr_ref[n, t].astype(F32) for n in range(n_dp)]
        for s in range(slots):
            col = ca_s[t, s // kmax, s % kmax]
            acc[col] += jnp.concatenate([v[:, s * rows:(s + 1) * rows] for v in sources], axis=1)
        return carry

    lax.fori_loop(0, n_t, group, 0)
    for b in range(blocks):
        gt_ref[:, b * blk:(b + 1) * blk] = acc[b].astype(BF16)
    put.wait()


def body(n_dp, n_t, tokens, weight_store, block_cols, block_count, block_home, grad_hidden):
    own, width = tokens.shape
    _, slots, rows, blk = weight_store.shape
    blocks = width // blk
    hb, kmax = block_cols.shape
    n_dev = n_dp * n_t
    group_rows = own * n_t
    groups = LANES // rows
    tiles = blocks // groups
    ff = hb * blk
    vmem = pl.BlockSpec(memory_space=pltpu.VMEM)
    smem = pl.BlockSpec(memory_space=pltpu.SMEM)
    place = pl.BlockSpec(memory_space=pl.ANY)
    dma = pltpu.SemaphoreType.DMA
    hid, wg, cr, ca = pl.pallas_call(
        functools.partial(exchange_kernel, n_dp, n_t),
        out_shape=(
            jax.ShapeDtypeStruct((group_rows, ff), BF16),
            jax.ShapeDtypeStruct((2, slots, rows, blk), BF16),
            jax.ShapeDtypeStruct((n_dp, n_t, own, slots * rows), BF16),
            jax.ShapeDtypeStruct((n_t, hb, kmax), jnp.int32),
        ),
        in_specs=[smem, smem, smem, vmem, vmem, place, vmem],
        out_specs=(place, place, place, place),
        scratch_shapes=[
            pltpu.VMEM((2, slots, rows, blk), BF16),
            pltpu.VMEM((n_dp, own, tiles, LANES), BF16),
            pltpu.VMEM((n_dp, n_t, own, tiles, LANES), BF16),
            pltpu.VMEM((blocks, rows, own * n_dev), F32),
            pltpu.VMEM((hb, kmax * rows, 2 * blk), BF16),
            pltpu.VMEM((hb, n_dp, group_rows, 2 * blk), BF16),
            pltpu.VMEM((hb, n_dp, group_rows, 2 * blk), BF16),
            pltpu.VMEM((hb, n_dp, group_rows, 2 * blk), BF16),
            pltpu.VMEM((n_dp, n_t, own, slots * rows), BF16),
            pltpu.VMEM((group_rows, ff), BF16),
            pltpu.VMEM((2, slots, rows, blk), BF16),
            dma((n_dp,)), dma((n_dp,)), dma((n_dp, n_t)), dma((n_dp, n_t)), dma((n_t,)), dma((n_t,)),
            dma((hb, n_dp)), dma((hb, n_dp)), dma((hb, n_dp)), dma((hb, n_dp)), dma((n_dp, n_t)), dma((n_dp, n_t)),
            dma((4,)),
        ],
        compiler_params=pltpu.CompilerParams(
            collective_id=0, has_side_effects=True, vmem_limit_bytes=60 * 1024 * 1024),
        name="exchange",
    )(block_cols, block_count, block_home, block_cols, tokens, weight_store, grad_hidden)
    return pl.pallas_call(
        place_kernel,
        out_shape=(
            jax.ShapeDtypeStruct((group_rows, ff), BF16),
            jax.ShapeDtypeStruct((own, width), BF16),
            jax.ShapeDtypeStruct((2, slots, rows, blk), BF16),
        ),
        in_specs=[vmem, smem, smem, vmem, place],
        out_specs=(vmem, vmem, place),
        scratch_shapes=[
            pltpu.VMEM((blocks, own, LANES), F32),
            pltpu.VMEM((2, slots, rows, blk), BF16),
            dma((slots,)), dma(()),
        ],
        compiler_params=pltpu.CompilerParams(vmem_limit_bytes=60 * 1024 * 1024),
        name="place",
    )(cr, ca, block_home, hid, wg)


def solution(mesh):
    return jax.shard_map(
        functools.partial(body, mesh.shape["dp"], mesh.shape["tensor"]),
        mesh=mesh,
        in_specs=(
            P(("dp", "tensor"), None),
            P(None, "tensor", "dp", None),
            P("tensor", None),
            P("tensor"),
            P("tensor", None),
            P("dp", "tensor"),
        ),
        out_specs=(P("dp", "tensor"), P(("dp", "tensor"), None), P(None, "tensor", "dp", None)),
        check_vma=False,
    )
```

```python
import functools
import jax
import jax.numpy as jnp
from jax import lax
from jax.experimental import pallas as pl
from jax.experimental.pallas import tpu as pltpu
from jax.sharding import PartitionSpec as P

MESH = pl.DeviceIdType.MESH
F32 = jnp.float32
BF16 = jnp.bfloat16
LANES = 128


def exchange_kernel(
    n_dp, n_t, cols_in, count_in, home_in, tok_in, w_hbm, gh_in,
    hid_out, wg_out, cr_ref, ca_ref,
    cols_s, count_s, home_s, cols_v, tok_ref, gh_ref,
    wv, tq, x, xt, wb, ps, pr, ga, c, hid_ref, wg_ref,
    s1, r1, s2, r2, sf, rf, sc, rc, sp, rp, sg, rg, st, rt, loc,
):
    n_dev = n_dp * n_t
    me_n, me_t = lax.axis_index("dp"), lax.axis_index("tensor")
    me = me_n * n_t + me_t
    own, width = tok_ref.shape
    rows = w_hbm.shape[2]
    blk = w_hbm.shape[3]
    blocks = width // blk
    hb, kmax = cols_s.shape
    groups = LANES // rows
    tiles = blocks // groups
    tokens = own * n_dev
    group_rows = own * n_t
    span = kmax * rows

    barrier = pltpu.get_barrier_semaphore()

    def greet(n, t):
        pl.semaphore_signal(barrier, inc=1, device_id=(n, t), device_id_type=MESH)

    def each(count, act, start=1):
        lax.fori_loop(start, count, lambda i, carry: (act(i), carry)[1], 0)

    each(n_t, lambda e: greet(me_n, lax.rem(me_t + e, n_t)))
    each(n_dp, lambda d: greet(lax.rem(me_n + d, n_dp), me_t))
    fetches = [
        pltpu.make_async_copy(src, dst, loc.at[4 + i])
        for i, (src, dst) in enumerate((
            (tok_in, tok_ref), (w_hbm, wv), (cols_in, cols_s), (count_in, count_s),
            (home_in, home_s), (cols_in, cols_v), (gh_in, gh_ref)))
    ]
    for fetch in fetches:
        fetch.start()
    fetches[0].wait()

    flat_tok = tok_ref[...].astype(F32)
    tok = jnp.stack([flat_tok[:, b * blk:(b + 1) * blk] for b in range(blocks)], axis=1)
    for n in range(n_dp):
        tq[n] = jnp.concatenate(
            [tok[:, g * tiles:(g + 1) * tiles, n * rows:(n + 1) * rows] for g in range(groups)], axis=2
        ).astype(BF16)
    for fetch in fetches[1:]:
        fetch.wait()
    for h in range(hb):
        for m in range(2):
            parts = []
            for k in range(kmax):
                keep = jnp.where(k < count_s[h], 1.0, 0.0).astype(F32)
                parts.append(wv[m, home_s[0, h * kmax + k]].astype(F32) * keep)
            wb[h, :, m * blk:(m + 1) * blk] = jnp.concatenate(parts, axis=0).astype(BF16)
    pl.semaphore_wait(barrier, n_dp + n_t - 2)

    chips = n_t // 2
    partner = me_t + 1 - 2 * lax.rem(me_t, 2)

    def ahead(d):
        return lax.rem(me_n + d, n_dp)

    def behind(d):
        return lax.rem(me_n - d + n_dp, n_dp)

    def first(d):
        n = ahead(d)
        return pltpu.make_async_remote_copy(
            src_ref=tq.at[n], dst_ref=x.at[me_n, me_t], send_sem=s1.at[d], recv_sem=r1.at[d],
            device_id=(n, me_t), device_id_type=MESH)

    def second(d, e):
        n, t = behind(d), lax.rem(me_t + 2 * e, n_t)
        return pltpu.make_async_remote_copy(
            src_ref=x.at[n, me_t], dst_ref=x.at[n, me_t], send_sem=s2.at[d, e], recv_sem=r2.at[d, e],
            device_id=(me_n, t), device_id_type=MESH)

    def share(d, e):
        n, t = behind(d), lax.rem(me_t - 2 * e + n_t, n_t)
        return pltpu.make_async_remote_copy(
            src_ref=x.at[n, t], dst_ref=x.at[n, t], send_sem=sf.at[d, e], recv_sem=rf.at[d, e],
            device_id=(me_n, partner), device_id_type=MESH)

    def columns(e):
        t = lax.rem(me_t + e, n_t)
        return pltpu.make_async_remote_copy(
            src_ref=cols_v, dst_ref=ca_ref.at[me_t], send_sem=sc.at[e], recv_sem=rc.at[e],
            device_id=(me_n, t), device_id_type=MESH)

    def partial(h, d):
        n = ahead(d)
        return pltpu.make_async_remote_copy(
            src_ref=ps.at[h, n], dst_ref=pr.at[h, d], send_sem=sp.at[h, d], recv_sem=rp.at[h, d],
            device_id=(n, me_t), device_id_type=MESH)

    def grads(h, d):
        n = ahead(d)
        return pltpu.make_async_remote_copy(
            src_ref=ga.at[h, me_n], dst_ref=ga.at[h, me_n], send_sem=sg.at[h, d], recv_sem=rg.at[h, d],
            device_id=(n, me_t), device_id_type=MESH)

    def terms(d, e):
        n, t = behind(d), lax.rem(me_t + e, n_t)
        return pltpu.make_async_remote_copy(
            src_ref=c.at[n, t], dst_ref=cr_ref.at[me_n, me_t], send_sem=st.at[d, e], recv_sem=rt.at[d, e],
            device_id=(n, t), device_id_type=MESH)

    each(n_dp, lambda d: first(d).start())
    own_tok = pltpu.make_async_copy(tq.at[me_n], x.at[me_n, me_t], loc.at[0])
    own_tok.start()
    own_cols = pltpu.make_async_copy(cols_v, ca_ref.at[me_t], loc.at[1])
    own_cols.start()
    own_tok.wait()

    def relay(d):
        each(chips, lambda e: second(d, e).start())
        share(d, 0).start()

    relay(0)
    each(n_dp, lambda d: (first(d).wait_recv(), relay(d)))
    each(n_t, lambda e: columns(e).start())

    def pass_on(d):
        def one(e):
            second(d, e).wait_recv()
            share(d, e).start()
        each(chips, one)

    each(n_dp, pass_on, 0)
    each(n_dp, lambda d: each(chips, lambda e: share(d, e).wait_recv(), 0), 0)

    flat = x[...].reshape(tokens, tiles, LANES).astype(F32)
    turned = jnp.swapaxes(flat, 0, 1)
    for j in range(tiles):
        upright = turned[j].T
        for g in range(groups):
            xt[g * tiles + j] = upright[g * rows:(g + 1) * rows]

    picked = []
    for h in range(hb):
        chosen = jnp.concatenate([xt[cols_s[h, k]] for k in range(kmax)], axis=0).astype(BF16)
        picked.append(chosen)
        pre = lax.dot_general(chosen, wb[h], (((0,), (0,)), ((), ())), preferred_element_type=F32)
        for n in range(n_dp):
            ps[h, n] = pre[n * group_rows:(n + 1) * group_rows].astype(BF16)
        each(n_dp, lambda d: partial(h, d).start())
    for h in range(hb):
        total = ps[h, me_n].astype(F32)
        each(n_dp, lambda d: partial(h, d).wait_recv())
        for d in range(1, n_dp):
            total = total + pr[h, d].astype(F32)
        gate, up = total[:, :blk], total[:, blk:]
        grad_in = gh_ref[:, h * blk:(h + 1) * blk].astype(F32)
        sigma = jax.nn.sigmoid(gate)
        act = gate * sigma
        hid_ref[:, h * blk:(h + 1) * blk] = (act * up).astype(BF16)
        ga[h, me_n] = jnp.concatenate(
            [grad_in * up * sigma * (1.0 + gate * (1.0 - sigma)), grad_in * act], axis=1).astype(BF16)
        each(n_dp, lambda d: grads(h, d).start())
    hid_copy = pltpu.make_async_copy(hid_ref, hid_out, loc.at[0])
    hid_copy.start()

    wide = -(-hb * span // LANES)

    def send_terms(n):
        parts = [
            lax.dot_general(ga[h, n], wb[h], (((1,), (1,)), ((), ())), preferred_element_type=F32)
            for h in range(hb)]
        if wide * LANES > hb * span:
            parts.append(jnp.zeros((group_rows, wide * LANES - hb * span), F32))
        part = jnp.concatenate(parts, axis=1)
        for t in range(n_t):
            c[n, t] = jnp.concatenate([
                part[t * own:(t + 1) * own, j * LANES:(j + 1) * LANES] for j in range(wide)], axis=0).astype(BF16)

    send_terms(me_n)
    own_terms = pltpu.make_async_copy(c.at[me_n, me_t], cr_ref.at[me_n, me_t], loc.at[2])
    own_terms.start()
    each(n_t, lambda e: terms(0, e).start())

    def others(d):
        for h in range(hb):
            grads(h, d).wait_recv()
        send_terms(behind(d))
        each(n_t, lambda e: terms(d, e).start(), 0)

    each(n_dp, others)

    for h in range(hb):
        every = jnp.concatenate([ga[h, n].astype(F32) for n in range(n_dp)], axis=0).astype(BF16)
        grown = jnp.dot(picked[h], every, preferred_element_type=F32)
        for k in range(kmax):
            keep = jnp.where(k < count_s[h], 1.0, 0.0).astype(F32)
            for m in range(2):
                wg_ref[m, h * kmax + k] = (
                    grown[k * rows:(k + 1) * rows, m * blk:(m + 1) * blk] * keep).astype(BF16)
    wg_copy = pltpu.make_async_copy(wg_ref, wg_out, loc.at[3])
    wg_copy.start()

    own_cols.wait()
    own_terms.wait()
    hid_copy.wait()
    each(n_t, lambda e: terms(0, e).wait_recv())
    each(n_dp, lambda d: each(n_t, lambda e: terms(d, e).wait_recv(), 0))
    each(n_t, lambda e: columns(e).wait_recv())
    each(n_dp, lambda d: first(d).wait_send())
    each(n_dp, lambda d: each(chips, lambda e: second(d, e).wait_send()), 0)
    each(n_dp, lambda d: each(chips, lambda e: share(d, e).wait_send(), 0), 0)
    each(n_t, lambda e: columns(e).wait_send())
    for h in range(hb):
        each(n_dp, lambda d: partial(h, d).wait_send())
        each(n_dp, lambda d: grads(h, d).wait_send())
    each(n_t, lambda e: terms(0, e).wait_send())
    each(n_dp, lambda d: each(n_t, lambda e: terms(d, e).wait_send(), 0))
    wg_copy.wait()


def place_kernel(cr_in, ca_s, home_s, hid_in, wg_in, hid_out, gt_ref, gw_out, acc, cr_ref, hid_ref, wv, fetched, other):
    n_dp, n_t, packed, _ = cr_in.shape
    rows, blk = wg_in.shape[2:]
    slots = wg_in.shape[1]
    hb, kmax = ca_s.shape[1:]
    blocks, own, _ = acc.shape
    groups = LANES // rows

    def fetch(s):
        return pltpu.make_async_copy(wg_in.at[:, s], wv.at[:, home_s[0, s]], fetched.at[s])

    cr_copy = pltpu.make_async_copy(cr_in, cr_ref, other.at[0])
    cr_copy.start()
    hid_copy = pltpu.make_async_copy(hid_in, hid_ref, other.at[1])
    hid_copy.start()
    for s in range(slots):
        fetch(s).start()
    acc[...] = jnp.zeros_like(acc)

    def group(t, carry):
        sources = [cr_ref[n, t].astype(F32) for n in range(n_dp)]
        mixed = [
            jnp.concatenate([v[:, g * rows:(g + 1) * rows] for v in sources], axis=1) for g in range(groups)]
        for h in range(hb):
            cols = [ca_s[t, h, k] for k in range(kmax)]
            held = [acc[col] for col in cols]
            for k in range(kmax):
                j, g = (h * kmax + k) // groups, (h * kmax + k) % groups
                acc[cols[k]] = held[k] + mixed[g][j * own:(j + 1) * own]
        return carry

    cr_copy.wait()
    lax.fori_loop(0, n_t // 2, group, 0)
    hid_copy.wait()
    hid_put = pltpu.make_async_copy(hid_ref, hid_out, other.at[2])
    hid_put.start()
    for s in range(slots):
        fetch(s).wait()
    put = pltpu.make_async_copy(wv, gw_out, other.at[3])
    put.start()
    lax.fori_loop(n_t // 2, n_t, group, 0)
    for b in range(blocks):
        gt_ref[:, b * blk:(b + 1) * blk] = acc[b].astype(BF16)
    hid_put.wait()
    put.wait()


def body(n_dp, n_t, tokens, weight_store, block_cols, block_count, block_home, grad_hidden):
    own, width = tokens.shape
    _, slots, rows, blk = weight_store.shape
    blocks = width // blk
    hb, kmax = block_cols.shape
    n_dev = n_dp * n_t
    group_rows = own * n_t
    groups = LANES // rows
    tiles = blocks // groups
    ff = hb * blk
    packed = own * -(-slots * rows // LANES)
    vmem = pl.BlockSpec(memory_space=pltpu.VMEM)
    smem = pl.BlockSpec(memory_space=pltpu.SMEM)
    place = pl.BlockSpec(memory_space=pl.ANY)
    dma = pltpu.SemaphoreType.DMA
    hid, wg, cr, ca = pl.pallas_call(
        functools.partial(exchange_kernel, n_dp, n_t),
        out_shape=(
            jax.ShapeDtypeStruct((group_rows, ff), BF16),
            jax.ShapeDtypeStruct((2, slots, rows, blk), BF16),
            jax.ShapeDtypeStruct((n_dp, n_t, packed, LANES), BF16),
            jax.ShapeDtypeStruct((n_t, hb, kmax), jnp.int32),
        ),
        in_specs=[place] * 6,
        out_specs=(place, place, place, place),
        scratch_shapes=[
            pltpu.SMEM((hb, kmax), jnp.int32),
            pltpu.SMEM((hb,), jnp.int32),
            pltpu.SMEM((1, slots), jnp.int32),
            pltpu.VMEM((hb, kmax), jnp.int32),
            pltpu.VMEM((own, width), BF16),
            pltpu.VMEM((group_rows, ff), BF16),
            pltpu.VMEM((2, slots, rows, blk), BF16),
            pltpu.VMEM((n_dp, own, tiles, LANES), BF16),
            pltpu.VMEM((n_dp, n_t, own, tiles, LANES), BF16),
            pltpu.VMEM((blocks, rows, own * n_dev), F32),
            pltpu.VMEM((hb, kmax * rows, 2 * blk), BF16),
            pltpu.VMEM((hb, n_dp, group_rows, 2 * blk), BF16),
            pltpu.VMEM((hb, n_dp, group_rows, 2 * blk), BF16),
            pltpu.VMEM((hb, n_dp, group_rows, 2 * blk), BF16),
            pltpu.VMEM((n_dp, n_t, packed, LANES), BF16),
            pltpu.VMEM((group_rows, ff), BF16),
            pltpu.VMEM((2, slots, rows, blk), BF16),
            dma((n_dp,)), dma((n_dp,)), dma((n_dp, n_t // 2)), dma((n_dp, n_t // 2)),
            dma((n_dp, n_t // 2)), dma((n_dp, n_t // 2)), dma((n_t,)), dma((n_t,)),
            dma((hb, n_dp)), dma((hb, n_dp)), dma((hb, n_dp)), dma((hb, n_dp)), dma((n_dp, n_t)), dma((n_dp, n_t)),
            dma((11,)),
        ],
        compiler_params=pltpu.CompilerParams(
            collective_id=0, has_side_effects=True, vmem_limit_bytes=60 * 1024 * 1024),
        name="exchange",
    )(block_cols, block_count, block_home, tokens, weight_store, grad_hidden)
    return pl.pallas_call(
        place_kernel,
        out_shape=(
            jax.ShapeDtypeStruct((group_rows, ff), BF16),
            jax.ShapeDtypeStruct((own, width), BF16),
            jax.ShapeDtypeStruct((2, slots, rows, blk), BF16),
        ),
        in_specs=[place, smem, smem, place, place],
        out_specs=(place, vmem, place),
        scratch_shapes=[
            pltpu.VMEM((blocks, own, LANES), F32),
            pltpu.VMEM((n_dp, n_t, packed, LANES), BF16),
            pltpu.VMEM((group_rows, ff), BF16),
            pltpu.VMEM((2, slots, rows, blk), BF16),
            dma((slots,)), dma((4,)),
        ],
        compiler_params=pltpu.CompilerParams(vmem_limit_bytes=60 * 1024 * 1024),
        name="place",
    )(cr, ca, block_home, hid, wg)


def solution(mesh):
    return jax.shard_map(
        functools.partial(body, mesh.shape["dp"], mesh.shape["tensor"]),
        mesh=mesh,
        in_specs=(
            P(("dp", "tensor"), None),
            P(None, "tensor", "dp", None),
            P("tensor", None),
            P("tensor"),
            P("tensor", None),
            P("dp", "tensor"),
        ),
        out_specs=(P("dp", "tensor"), P(("dp", "tensor"), None), P(None, "tensor", "dp", None)),
        check_vma=False,
    )
```

```python
import functools
import jax
import jax.numpy as jnp
from jax import lax
from jax.experimental import pallas as pl
from jax.experimental.pallas import tpu as pltpu
from jax.sharding import PartitionSpec as P

MESH = pl.DeviceIdType.MESH
F32 = jnp.float32
BF16 = jnp.bfloat16
LANES = 128


def exchange_kernel(
    n_dp, n_t, cols_in, count_in, home_in, tok_in, w_hbm, gh_in,
    hid_out, wg_out, cr_ref, ca_ref,
    cols_s, count_s, home_s, cols_v, tok_ref, gh_ref,
    wv, tq, x, xt, wb, ps, pr, ga, c, hid_ref, wg_ref,
    s1, r1, s2, r2, sf, rf, sc, rc, sp, rp, sg, rg, st, rt, loc,
):
    n_dev = n_dp * n_t
    me_n, me_t = lax.axis_index("dp"), lax.axis_index("tensor")
    me = me_n * n_t + me_t
    own, width = tok_ref.shape
    rows = w_hbm.shape[2]
    blk = w_hbm.shape[3]
    blocks = width // blk
    hb, kmax = cols_s.shape
    groups = LANES // rows
    tiles = blocks // groups
    tokens = own * n_dev
    group_rows = own * n_t
    span = kmax * rows

    barrier = pltpu.get_barrier_semaphore()

    def greet(n, t):
        pl.semaphore_signal(barrier, inc=1, device_id=(n, t), device_id_type=MESH)

    def each(count, act, start=1):
        lax.fori_loop(start, count, lambda i, carry: (act(i), carry)[1], 0)

    each(n_t, lambda e: greet(me_n, lax.rem(me_t + e, n_t)))
    each(n_dp, lambda d: greet(lax.rem(me_n + d, n_dp), me_t))
    fetches = [
        pltpu.make_async_copy(src, dst, loc.at[4 + i])
        for i, (src, dst) in enumerate((
            (tok_in, tok_ref), (w_hbm, wv), (cols_in, cols_s), (count_in, count_s),
            (home_in, home_s), (cols_in, cols_v), (gh_in, gh_ref)))
    ]
    for fetch in fetches:
        fetch.start()
    fetches[0].wait()

    flat_tok = tok_ref[...].astype(F32)
    tok = jnp.stack([flat_tok[:, b * blk:(b + 1) * blk] for b in range(blocks)], axis=1)
    for n in range(n_dp):
        tq[n] = jnp.concatenate(
            [tok[:, g * tiles:(g + 1) * tiles, n * rows:(n + 1) * rows] for g in range(groups)], axis=2
        ).astype(BF16)
    for fetch in fetches[1:]:
        fetch.wait()
    for h in range(hb):
        for m in range(2):
            parts = []
            for k in range(kmax):
                keep = jnp.where(k < count_s[h], 1.0, 0.0).astype(F32)
                parts.append(wv[m, home_s[0, h * kmax + k]].astype(F32) * keep)
            wb[h, :, m * blk:(m + 1) * blk] = jnp.concatenate(parts, axis=0).astype(BF16)
    pl.semaphore_wait(barrier, n_dp + n_t - 2)

    chips = n_t // 2
    partner = me_t + 1 - 2 * lax.rem(me_t, 2)

    def paired(d):
        if n_dp & (n_dp - 1):
            return lax.rem(me_n + d, n_dp), lax.rem(me_n - d + n_dp, n_dp)
        mate, bit = 0, 1
        while bit < n_dp:
            mate += lax.rem(me_n // bit + d // bit, 2) * bit
            bit *= 2
        return mate, mate

    def ahead(d):
        return paired(d)[0]

    def behind(d):
        return paired(d)[1]

    def first(d):
        n = ahead(d)
        return pltpu.make_async_remote_copy(
            src_ref=tq.at[n], dst_ref=x.at[me_n, me_t], send_sem=s1.at[d], recv_sem=r1.at[d],
            device_id=(n, me_t), device_id_type=MESH)

    def second(d, e):
        n, t = behind(d), lax.rem(me_t + 2 * e, n_t)
        return pltpu.make_async_remote_copy(
            src_ref=x.at[n, me_t], dst_ref=x.at[n, me_t], send_sem=s2.at[d, e], recv_sem=r2.at[d, e],
            device_id=(me_n, t), device_id_type=MESH)

    def share(d, e):
        n, t = behind(d), lax.rem(me_t - 2 * e + n_t, n_t)
        return pltpu.make_async_remote_copy(
            src_ref=x.at[n, t], dst_ref=x.at[n, t], send_sem=sf.at[d, e], recv_sem=rf.at[d, e],
            device_id=(me_n, partner), device_id_type=MESH)

    def columns(e):
        t = lax.rem(me_t + e, n_t)
        return pltpu.make_async_remote_copy(
            src_ref=cols_v, dst_ref=ca_ref.at[me_t], send_sem=sc.at[e], recv_sem=rc.at[e],
            device_id=(me_n, t), device_id_type=MESH)

    def partial(h, d):
        n = ahead(d)
        return pltpu.make_async_remote_copy(
            src_ref=ps.at[h, n], dst_ref=pr.at[h, d], send_sem=sp.at[h, d], recv_sem=rp.at[h, d],
            device_id=(n, me_t), device_id_type=MESH)

    def grads(h, d):
        n = ahead(d)
        return pltpu.make_async_remote_copy(
            src_ref=ga.at[h, me_n], dst_ref=ga.at[h, me_n], send_sem=sg.at[h, d], recv_sem=rg.at[h, d],
            device_id=(n, me_t), device_id_type=MESH)

    def terms(d, e):
        n, t = behind(d), lax.rem(me_t + e, n_t)
        return pltpu.make_async_remote_copy(
            src_ref=c.at[n, t], dst_ref=cr_ref.at[me_n, me_t], send_sem=st.at[d, e], recv_sem=rt.at[d, e],
            device_id=(n, t), device_id_type=MESH)

    each(n_dp, lambda d: first(d).start())
    own_tok = pltpu.make_async_copy(tq.at[me_n], x.at[me_n, me_t], loc.at[0])
    own_tok.start()
    own_cols = pltpu.make_async_copy(cols_v, ca_ref.at[me_t], loc.at[1])
    own_cols.start()
    own_tok.wait()

    def relay(d):
        each(chips, lambda e: second(d, e).start())
        share(d, 0).start()

    relay(0)
    each(n_dp, lambda d: (first(d).wait_recv(), relay(d)))
    each(n_t, lambda e: columns(e).start())

    def pass_on(d):
        def one(e):
            second(d, e).wait_recv()
            share(d, e).start()
        each(chips, one)

    each(n_dp, pass_on, 0)
    each(n_dp, lambda d: each(chips, lambda e: share(d, e).wait_recv(), 0), 0)

    flat = x[...].reshape(tokens, tiles, LANES).astype(F32)
    turned = jnp.swapaxes(flat, 0, 1)
    for j in range(tiles):
        upright = turned[j].T
        for g in range(groups):
            xt[g * tiles + j] = upright[g * rows:(g + 1) * rows]

    picked = []
    for h in range(hb):
        chosen = jnp.concatenate([xt[cols_s[h, k]] for k in range(kmax)], axis=0).astype(BF16)
        picked.append(chosen)
        pre = lax.dot_general(chosen, wb[h], (((0,), (0,)), ((), ())), preferred_element_type=F32)
        for n in range(n_dp):
            ps[h, n] = pre[n * group_rows:(n + 1) * group_rows].astype(BF16)
        each(n_dp, lambda d: partial(h, d).start())
    for h in range(hb):
        total = ps[h, me_n].astype(F32)
        each(n_dp, lambda d: partial(h, d).wait_recv())
        for d in range(1, n_dp):
            total = total + pr[h, d].astype(F32)
        gate, up = total[:, :blk], total[:, blk:]
        grad_in = gh_ref[:, h * blk:(h + 1) * blk].astype(F32)
        sigma = jax.nn.sigmoid(gate)
        act = gate * sigma
        hid_ref[:, h * blk:(h + 1) * blk] = (act * up).astype(BF16)
        ga[h, me_n] = jnp.concatenate(
            [grad_in * up * sigma * (1.0 + gate * (1.0 - sigma)), grad_in * act], axis=1).astype(BF16)
        each(n_dp, lambda d: grads(h, d).start())
    hid_copy = pltpu.make_async_copy(hid_ref, hid_out, loc.at[0])
    hid_copy.start()

    wide = -(-hb * span // LANES)

    def send_terms(n):
        parts = [
            lax.dot_general(ga[h, n], wb[h], (((1,), (1,)), ((), ())), preferred_element_type=F32)
            for h in range(hb)]
        if wide * LANES > hb * span:
            parts.append(jnp.zeros((group_rows, wide * LANES - hb * span), F32))
        part = jnp.concatenate(parts, axis=1)
        for t in range(n_t):
            c[n, t] = jnp.concatenate([
                part[t * own:(t + 1) * own, j * LANES:(j + 1) * LANES] for j in range(wide)], axis=0).astype(BF16)

    send_terms(me_n)
    own_terms = pltpu.make_async_copy(c.at[me_n, me_t], cr_ref.at[me_n, me_t], loc.at[2])
    own_terms.start()
    each(n_t, lambda e: terms(0, e).start())

    def others(d):
        for h in range(hb):
            grads(h, d).wait_recv()
        send_terms(behind(d))
        each(n_t, lambda e: terms(d, e).start(), 0)

    each(n_dp, others)

    for h in range(hb):
        every = jnp.concatenate([ga[h, n].astype(F32) for n in range(n_dp)], axis=0).astype(BF16)
        grown = jnp.dot(picked[h], every, preferred_element_type=F32)
        for k in range(kmax):
            keep = jnp.where(k < count_s[h], 1.0, 0.0).astype(F32)
            for m in range(2):
                wg_ref[m, h * kmax + k] = (
                    grown[k * rows:(k + 1) * rows, m * blk:(m + 1) * blk] * keep).astype(BF16)
    wg_copy = pltpu.make_async_copy(wg_ref, wg_out, loc.at[3])
    wg_copy.start()

    own_cols.wait()
    own_terms.wait()
    hid_copy.wait()
    each(n_t, lambda e: terms(0, e).wait_recv())
    each(n_dp, lambda d: each(n_t, lambda e: terms(d, e).wait_recv(), 0))
    each(n_t, lambda e: columns(e).wait_recv())
    each(n_dp, lambda d: first(d).wait_send())
    each(n_dp, lambda d: each(chips, lambda e: second(d, e).wait_send()), 0)
    each(n_dp, lambda d: each(chips, lambda e: share(d, e).wait_send(), 0), 0)
    each(n_t, lambda e: columns(e).wait_send())
    for h in range(hb):
        each(n_dp, lambda d: partial(h, d).wait_send())
        each(n_dp, lambda d: grads(h, d).wait_send())
    each(n_t, lambda e: terms(0, e).wait_send())
    each(n_dp, lambda d: each(n_t, lambda e: terms(d, e).wait_send(), 0))
    wg_copy.wait()


def place_kernel(
    cr_in, ca_in, home_in, hid_in, wg_in, hid_out, gt_ref, gw_out,
    acc, cr_ref, hid_ref, wv, ca_s, home_s, fetched, other,
):
    n_dp, n_t, packed, _ = cr_in.shape
    rows, blk = wg_in.shape[2:]
    slots = wg_in.shape[1]
    hb, kmax = ca_s.shape[1:]
    blocks, own, _ = acc.shape
    groups = LANES // rows

    def fetch(s):
        return pltpu.make_async_copy(wg_in.at[:, s], wv.at[:, home_s[0, s]], fetched.at[s])

    home_copy = pltpu.make_async_copy(home_in, home_s, other.at[4])
    home_copy.start()
    ca_copy = pltpu.make_async_copy(ca_in, ca_s, other.at[5])
    ca_copy.start()
    cr_copy = pltpu.make_async_copy(cr_in, cr_ref, other.at[0])
    cr_copy.start()
    hid_copy = pltpu.make_async_copy(hid_in, hid_ref, other.at[1])
    hid_copy.start()
    acc[...] = jnp.zeros_like(acc)
    home_copy.wait()
    for s in range(slots):
        fetch(s).start()

    def group(t, carry):
        sources = [cr_ref[n, t].astype(F32) for n in range(n_dp)]
        mixed = [
            jnp.concatenate([v[:, g * rows:(g + 1) * rows] for v in sources], axis=1) for g in range(groups)]
        for h in range(hb):
            cols = [ca_s[t, h, k] for k in range(kmax)]
            held = [acc[col] for col in cols]
            for k in range(kmax):
                j, g = (h * kmax + k) // groups, (h * kmax + k) % groups
                acc[cols[k]] = held[k] + mixed[g][j * own:(j + 1) * own]
        return carry

    ca_copy.wait()
    cr_copy.wait()
    lax.fori_loop(0, n_t // 2, group, 0)
    hid_copy.wait()
    hid_put = pltpu.make_async_copy(hid_ref, hid_out, other.at[2])
    hid_put.start()
    for s in range(slots):
        fetch(s).wait()
    put = pltpu.make_async_copy(wv, gw_out, other.at[3])
    put.start()
    lax.fori_loop(n_t // 2, n_t, group, 0)
    for b in range(blocks):
        gt_ref[:, b * blk:(b + 1) * blk] = acc[b].astype(BF16)
    hid_put.wait()
    put.wait()


def body(n_dp, n_t, tokens, weight_store, block_cols, block_count, block_home, grad_hidden):
    own, width = tokens.shape
    _, slots, rows, blk = weight_store.shape
    blocks = width // blk
    hb, kmax = block_cols.shape
    n_dev = n_dp * n_t
    group_rows = own * n_t
    groups = LANES // rows
    tiles = blocks // groups
    ff = hb * blk
    packed = own * -(-slots * rows // LANES)
    vmem = pl.BlockSpec(memory_space=pltpu.VMEM)
    place = pl.BlockSpec(memory_space=pl.ANY)
    dma = pltpu.SemaphoreType.DMA
    hid, wg, cr, ca = pl.pallas_call(
        functools.partial(exchange_kernel, n_dp, n_t),
        out_shape=(
            jax.ShapeDtypeStruct((group_rows, ff), BF16),
            jax.ShapeDtypeStruct((2, slots, rows, blk), BF16),
            jax.ShapeDtypeStruct((n_dp, n_t, packed, LANES), BF16),
            jax.ShapeDtypeStruct((n_t, hb, kmax), jnp.int32),
        ),
        in_specs=[place] * 6,
        out_specs=(place, place, place, place),
        scratch_shapes=[
            pltpu.SMEM((hb, kmax), jnp.int32),
            pltpu.SMEM((hb,), jnp.int32),
            pltpu.SMEM((1, slots), jnp.int32),
            pltpu.VMEM((hb, kmax), jnp.int32),
            pltpu.VMEM((own, width), BF16),
            pltpu.VMEM((group_rows, ff), BF16),
            pltpu.VMEM((2, slots, rows, blk), BF16),
            pltpu.VMEM((n_dp, own, tiles, LANES), BF16),
            pltpu.VMEM((n_dp, n_t, own, tiles, LANES), BF16),
            pltpu.VMEM((blocks, rows, own * n_dev), F32),
            pltpu.VMEM((hb, kmax * rows, 2 * blk), BF16),
            pltpu.VMEM((hb, n_dp, group_rows, 2 * blk), BF16),
            pltpu.VMEM((hb, n_dp, group_rows, 2 * blk), BF16),
            pltpu.VMEM((hb, n_dp, group_rows, 2 * blk), BF16),
            pltpu.VMEM((n_dp, n_t, packed, LANES), BF16),
            pltpu.VMEM((group_rows, ff), BF16),
            pltpu.VMEM((2, slots, rows, blk), BF16),
            dma((n_dp,)), dma((n_dp,)), dma((n_dp, n_t // 2)), dma((n_dp, n_t // 2)),
            dma((n_dp, n_t // 2)), dma((n_dp, n_t // 2)), dma((n_t,)), dma((n_t,)),
            dma((hb, n_dp)), dma((hb, n_dp)), dma((hb, n_dp)), dma((hb, n_dp)), dma((n_dp, n_t)), dma((n_dp, n_t)),
            dma((11,)),
        ],
        compiler_params=pltpu.CompilerParams(
            collective_id=0, has_side_effects=True, vmem_limit_bytes=60 * 1024 * 1024),
        name="exchange",
    )(block_cols, block_count, block_home, tokens, weight_store, grad_hidden)
    return pl.pallas_call(
        place_kernel,
        out_shape=(
            jax.ShapeDtypeStruct((group_rows, ff), BF16),
            jax.ShapeDtypeStruct((own, width), BF16),
            jax.ShapeDtypeStruct((2, slots, rows, blk), BF16),
        ),
        in_specs=[place] * 5,
        out_specs=(place, vmem, place),
        scratch_shapes=[
            pltpu.VMEM((blocks, own, LANES), F32),
            pltpu.VMEM((n_dp, n_t, packed, LANES), BF16),
            pltpu.VMEM((group_rows, ff), BF16),
            pltpu.VMEM((2, slots, rows, blk), BF16),
            pltpu.SMEM((n_t, hb, kmax), jnp.int32),
            pltpu.SMEM((1, slots), jnp.int32),
            dma((slots,)), dma((6,)),
        ],
        compiler_params=pltpu.CompilerParams(vmem_limit_bytes=60 * 1024 * 1024),
        name="place",
    )(cr, ca, block_home, hid, wg)


def solution(mesh):
    return jax.shard_map(
        functools.partial(body, mesh.shape["dp"], mesh.shape["tensor"]),
        mesh=mesh,
        in_specs=(
            P(("dp", "tensor"), None),
            P(None, "tensor", "dp", None),
            P("tensor", None),
            P("tensor"),
            P("tensor", None),
            P("dp", "tensor"),
        ),
        out_specs=(P("dp", "tensor"), P(("dp", "tensor"), None), P(None, "tensor", "dp", None)),
        check_vma=False,
    )
```

```python
import functools
import jax
import jax.numpy as jnp
from jax import lax
from jax.experimental import pallas as pl
from jax.experimental.pallas import tpu as pltpu
from jax.sharding import PartitionSpec as P

MESH = pl.DeviceIdType.MESH
F32 = jnp.float32
BF16 = jnp.bfloat16
LANES = 128


def exchange_kernel(
    n_dp, n_t, cols_in, count_in, home_in, tok_in, w_hbm, gh_in,
    hid_out, wg_out, cr_ref, ca_ref,
    cols_s, count_s, home_s, cols_v, tok_ref, gh_ref,
    wv, tq, x, xt, wb, ps, pr, ga, c, hid_ref, wg_ref,
    s1, r1, s2, r2, sf, rf, sc, rc, sp, rp, sg, rg, st, rt, loc,
):
    n_dev = n_dp * n_t
    me_n, me_t = lax.axis_index("dp"), lax.axis_index("tensor")
    me = me_n * n_t + me_t
    own, width = tok_ref.shape
    rows = w_hbm.shape[2]
    blk = w_hbm.shape[3]
    blocks = width // blk
    hb, kmax = cols_s.shape
    groups = LANES // rows
    tiles = blocks // groups
    tokens = own * n_dev
    group_rows = own * n_t
    span = kmax * rows

    barrier = pltpu.get_barrier_semaphore()

    def greet(n, t):
        pl.semaphore_signal(barrier, inc=1, device_id=(n, t), device_id_type=MESH)

    def each(count, act, start=1):
        lax.fori_loop(start, count, lambda i, carry: (act(i), carry)[1], 0)

    each(n_t, lambda e: greet(me_n, lax.rem(me_t + e, n_t)))
    each(n_dp, lambda d: greet(lax.rem(me_n + d, n_dp), me_t))
    fetches = [
        pltpu.make_async_copy(src, dst, loc.at[4 + i])
        for i, (src, dst) in enumerate((
            (tok_in, tok_ref), (w_hbm, wv), (cols_in, cols_s), (count_in, count_s),
            (home_in, home_s), (cols_in, cols_v), (gh_in, gh_ref)))
    ]
    for fetch in fetches:
        fetch.start()
    fetches[0].wait()

    flat_tok = tok_ref[...].astype(F32)
    tok = jnp.stack([flat_tok[:, b * blk:(b + 1) * blk] for b in range(blocks)], axis=1)
    for n in range(n_dp):
        tq[n] = jnp.concatenate(
            [tok[:, g * tiles:(g + 1) * tiles, n * rows:(n + 1) * rows] for g in range(groups)], axis=2
        ).astype(BF16)
    for fetch in fetches[1:]:
        fetch.wait()
    for h in range(hb):
        for m in range(2):
            parts = []
            for k in range(kmax):
                keep = jnp.where(k < count_s[h], 1.0, 0.0).astype(F32)
                parts.append(wv[m, home_s[0, h * kmax + k]].astype(F32) * keep)
            wb[h, :, m * blk:(m + 1) * blk] = jnp.concatenate(parts, axis=0).astype(BF16)
    pl.semaphore_wait(barrier, n_dp + n_t - 2)

    chips = n_t // 2
    partner = me_t + 1 - 2 * lax.rem(me_t, 2)

    def paired(d):
        if n_dp & (n_dp - 1):
            return lax.rem(me_n + d, n_dp), lax.rem(me_n - d + n_dp, n_dp)
        mate, bit = 0, 1
        while bit < n_dp:
            mate += lax.rem(me_n // bit + d // bit, 2) * bit
            bit *= 2
        return mate, mate

    def ahead(d):
        return paired(d)[0]

    def behind(d):
        return paired(d)[1]

    def first(d):
        n = ahead(d)
        return pltpu.make_async_remote_copy(
            src_ref=tq.at[n], dst_ref=x.at[me_n, me_t], send_sem=s1.at[d], recv_sem=r1.at[d],
            device_id=(n, me_t), device_id_type=MESH)

    def second(d, e):
        n, t = behind(d), lax.rem(me_t + 2 * e, n_t)
        return pltpu.make_async_remote_copy(
            src_ref=x.at[n, me_t], dst_ref=x.at[n, me_t], send_sem=s2.at[d, e], recv_sem=r2.at[d, e],
            device_id=(me_n, t), device_id_type=MESH)

    def share(d, e):
        n, t = behind(d), lax.rem(me_t - 2 * e + n_t, n_t)
        return pltpu.make_async_remote_copy(
            src_ref=x.at[n, t], dst_ref=x.at[n, t], send_sem=sf.at[d, e], recv_sem=rf.at[d, e],
            device_id=(me_n, partner), device_id_type=MESH)

    def columns(e):
        t = lax.rem(me_t + e, n_t)
        return pltpu.make_async_remote_copy(
            src_ref=cols_v, dst_ref=ca_ref.at[me_t], send_sem=sc.at[e], recv_sem=rc.at[e],
            device_id=(me_n, t), device_id_type=MESH)

    def partial(h, d):
        n = ahead(d)
        return pltpu.make_async_remote_copy(
            src_ref=ps.at[h, n], dst_ref=pr.at[h, d], send_sem=sp.at[h, d], recv_sem=rp.at[h, d],
            device_id=(n, me_t), device_id_type=MESH)

    def grads(h, d):
        n = ahead(d)
        return pltpu.make_async_remote_copy(
            src_ref=ga.at[h, me_n], dst_ref=ga.at[h, me_n], send_sem=sg.at[h, d], recv_sem=rg.at[h, d],
            device_id=(n, me_t), device_id_type=MESH)

    def terms(d, e):
        n, t = behind(d), lax.rem(me_t + e, n_t)
        return pltpu.make_async_remote_copy(
            src_ref=c.at[n, t], dst_ref=cr_ref.at[me_n, me_t], send_sem=st.at[d, e], recv_sem=rt.at[d, e],
            device_id=(n, t), device_id_type=MESH)

    each(n_dp, lambda d: first(d).start())
    own_tok = pltpu.make_async_copy(tq.at[me_n], x.at[me_n, me_t], loc.at[0])
    own_tok.start()
    own_cols = pltpu.make_async_copy(cols_v, ca_ref.at[me_t], loc.at[1])
    own_cols.start()
    own_tok.wait()

    def relay(d):
        each(chips, lambda e: second(d, e).start())
        share(d, 0).start()

    relay(0)
    each(n_dp, lambda d: (first(d).wait_recv(), relay(d)))
    each(n_t, lambda e: columns(e).start())

    def pass_on(d):
        def one(e):
            second(d, e).wait_recv()
            share(d, e).start()
        each(chips, one)

    each(n_dp, pass_on, 0)
    each(n_dp, lambda d: each(chips, lambda e: share(d, e).wait_recv(), 0), 0)

    flat = x[...].reshape(tokens, tiles, LANES).astype(F32)
    turned = jnp.swapaxes(flat, 0, 1)
    for j in range(tiles):
        upright = turned[j].T
        for g in range(groups):
            xt[g * tiles + j] = upright[g * rows:(g + 1) * rows]

    picked = []
    for h in range(hb):
        chosen = jnp.concatenate([xt[cols_s[h, k]] for k in range(kmax)], axis=0).astype(BF16)
        picked.append(chosen)
        pre = lax.dot_general(chosen, wb[h], (((0,), (0,)), ((), ())), preferred_element_type=F32)
        for n in range(n_dp):
            ps[h, n] = pre[n * group_rows:(n + 1) * group_rows].astype(BF16)
        each(n_dp, lambda d: partial(h, d).start())
    for h in range(hb):
        total = ps[h, me_n].astype(F32)
        each(n_dp, lambda d: partial(h, d).wait_recv())
        for d in range(1, n_dp):
            total = total + pr[h, d].astype(F32)
        gate, up = total[:, :blk], total[:, blk:]
        grad_in = gh_ref[:, h * blk:(h + 1) * blk].astype(F32)
        sigma = jax.nn.sigmoid(gate)
        act = gate * sigma
        hid_ref[:, h * blk:(h + 1) * blk] = (act * up).astype(BF16)
        ga[h, me_n] = jnp.concatenate(
            [grad_in * up * sigma * (1.0 + gate * (1.0 - sigma)), grad_in * act], axis=1).astype(BF16)
        each(n_dp, lambda d: grads(h, d).start())
    hid_copy = pltpu.make_async_copy(hid_ref, hid_out, loc.at[0])
    hid_copy.start()

    wide = -(-hb * span // LANES)

    def send_terms(n):
        parts = [
            lax.dot_general(ga[h, n], wb[h], (((1,), (1,)), ((), ())), preferred_element_type=F32)
            for h in range(hb)]
        if wide * LANES > hb * span:
            parts.append(jnp.zeros((group_rows, wide * LANES - hb * span), F32))
        part = jnp.concatenate(parts, axis=1)
        for t in range(n_t):
            c[n, t] = jnp.concatenate([
                part[t * own:(t + 1) * own, j * LANES:(j + 1) * LANES] for j in range(wide)], axis=0).astype(BF16)

    send_terms(me_n)
    own_terms = pltpu.make_async_copy(c.at[me_n, me_t], cr_ref.at[me_n, me_t], loc.at[2])
    own_terms.start()
    each(n_t, lambda e: terms(0, e).start())

    def others(d):
        for h in range(hb):
            grads(h, d).wait_recv()
        send_terms(behind(d))
        each(n_t, lambda e: terms(d, e).start(), 0)

    each(n_dp, others)

    for h in range(hb):
        every = jnp.concatenate([ga[h, n].astype(F32) for n in range(n_dp)], axis=0).astype(BF16)
        grown = jnp.dot(picked[h], every, preferred_element_type=F32)
        for k in range(kmax):
            keep = jnp.where(k < count_s[h], 1.0, 0.0).astype(F32)
            for m in range(2):
                wg_ref[m, h * kmax + k] = (
                    grown[k * rows:(k + 1) * rows, m * blk:(m + 1) * blk] * keep).astype(BF16)
    wg_copy = pltpu.make_async_copy(wg_ref, wg_out, loc.at[3])
    wg_copy.start()

    own_cols.wait()
    own_terms.wait()
    hid_copy.wait()
    each(n_t, lambda e: columns(e).wait_recv())
    each(n_dp, lambda d: first(d).wait_send())
    each(n_dp, lambda d: each(chips, lambda e: second(d, e).wait_send()), 0)
    each(n_dp, lambda d: each(chips, lambda e: share(d, e).wait_send(), 0), 0)
    each(n_t, lambda e: columns(e).wait_send())
    for h in range(hb):
        each(n_dp, lambda d: partial(h, d).wait_send())
        each(n_dp, lambda d: grads(h, d).wait_send())
    each(n_t, lambda e: terms(0, e).wait_send())
    each(n_dp, lambda d: each(n_t, lambda e: terms(d, e).wait_send(), 0))
    wg_copy.wait()
    each(n_t, lambda e: terms(0, e).wait_recv())
    each(n_dp, lambda d: each(n_t, lambda e: terms(d, e).wait_recv(), 0))


def place_kernel(
    cr_in, ca_in, home_in, hid_in, wg_in, hid_out, gt_ref, gw_out,
    acc, cr_ref, hid_ref, wv, ca_s, home_s, fetched, other,
):
    n_dp, n_t, packed, _ = cr_in.shape
    rows, blk = wg_in.shape[2:]
    slots = wg_in.shape[1]
    hb, kmax = ca_s.shape[1:]
    blocks, own, _ = acc.shape
    groups = LANES // rows

    def fetch(s):
        return pltpu.make_async_copy(wg_in.at[:, s], wv.at[:, home_s[0, s]], fetched.at[s])

    home_copy = pltpu.make_async_copy(home_in, home_s, other.at[4])
    home_copy.start()
    ca_copy = pltpu.make_async_copy(ca_in, ca_s, other.at[5])
    ca_copy.start()
    cr_copy = pltpu.make_async_copy(cr_in, cr_ref, other.at[0])
    cr_copy.start()
    hid_copy = pltpu.make_async_copy(hid_in, hid_ref, other.at[1])
    hid_copy.start()
    acc[...] = jnp.zeros_like(acc)
    home_copy.wait()
    for s in range(slots):
        fetch(s).start()

    def group(t, carry):
        sources = [cr_ref[n, t].astype(F32) for n in range(n_dp)]
        mixed = [
            jnp.concatenate([v[:, g * rows:(g + 1) * rows] for v in sources], axis=1) for g in range(groups)]
        for h in range(hb):
            cols = [ca_s[t, h, k] for k in range(kmax)]
            held = [acc[col] for col in cols]
            for k in range(kmax):
                j, g = (h * kmax + k) // groups, (h * kmax + k) % groups
                acc[cols[k]] = held[k] + mixed[g][j * own:(j + 1) * own]
        return carry

    ca_copy.wait()
    cr_copy.wait()
    lax.fori_loop(0, n_t // 2, group, 0)
    hid_copy.wait()
    hid_put = pltpu.make_async_copy(hid_ref, hid_out, other.at[2])
    hid_put.start()
    for s in range(slots):
        fetch(s).wait()
    put = pltpu.make_async_copy(wv, gw_out, other.at[3])
    put.start()
    lax.fori_loop(n_t // 2, n_t, group, 0)
    for b in range(blocks):
        gt_ref[:, b * blk:(b + 1) * blk] = acc[b].astype(BF16)
    hid_put.wait()
    put.wait()


def body(n_dp, n_t, tokens, weight_store, block_cols, block_count, block_home, grad_hidden):
    own, width = tokens.shape
    _, slots, rows, blk = weight_store.shape
    blocks = width // blk
    hb, kmax = block_cols.shape
    n_dev = n_dp * n_t
    group_rows = own * n_t
    groups = LANES // rows
    tiles = blocks // groups
    ff = hb * blk
    packed = own * -(-slots * rows // LANES)
    vmem = pl.BlockSpec(memory_space=pltpu.VMEM)
    place = pl.BlockSpec(memory_space=pl.ANY)
    dma = pltpu.SemaphoreType.DMA
    hid, wg, cr, ca = pl.pallas_call(
        functools.partial(exchange_kernel, n_dp, n_t),
        out_shape=(
            jax.ShapeDtypeStruct((group_rows, ff), BF16),
            jax.ShapeDtypeStruct((2, slots, rows, blk), BF16),
            jax.ShapeDtypeStruct((n_dp, n_t, packed, LANES), BF16),
            jax.ShapeDtypeStruct((n_t, hb, kmax), jnp.int32),
        ),
        in_specs=[place] * 6,
        out_specs=(place, place, place, place),
        scratch_shapes=[
            pltpu.SMEM((hb, kmax), jnp.int32),
            pltpu.SMEM((hb,), jnp.int32),
            pltpu.SMEM((1, slots), jnp.int32),
            pltpu.VMEM((hb, kmax), jnp.int32),
            pltpu.VMEM((own, width), BF16),
            pltpu.VMEM((group_rows, ff), BF16),
            pltpu.VMEM((2, slots, rows, blk), BF16),
            pltpu.VMEM((n_dp, own, tiles, LANES), BF16),
            pltpu.VMEM((n_dp, n_t, own, tiles, LANES), BF16),
            pltpu.VMEM((blocks, rows, own * n_dev), F32),
            pltpu.VMEM((hb, kmax * rows, 2 * blk), BF16),
            pltpu.VMEM((hb, n_dp, group_rows, 2 * blk), BF16),
            pltpu.VMEM((hb, n_dp, group_rows, 2 * blk), BF16),
            pltpu.VMEM((hb, n_dp, group_rows, 2 * blk), BF16),
            pltpu.VMEM((n_dp, n_t, packed, LANES), BF16),
            pltpu.VMEM((group_rows, ff), BF16),
            pltpu.VMEM((2, slots, rows, blk), BF16),
            dma((n_dp,)), dma((n_dp,)), dma((n_dp, n_t // 2)), dma((n_dp, n_t // 2)),
            dma((n_dp, n_t // 2)), dma((n_dp, n_t // 2)), dma((n_t,)), dma((n_t,)),
            dma((hb, n_dp)), dma((hb, n_dp)), dma((hb, n_dp)), dma((hb, n_dp)), dma((n_dp, n_t)), dma((n_dp, n_t)),
            dma((11,)),
        ],
        compiler_params=pltpu.CompilerParams(
            collective_id=0, has_side_effects=True, vmem_limit_bytes=60 * 1024 * 1024),
        name="exchange",
    )(block_cols, block_count, block_home, tokens, weight_store, grad_hidden)
    return pl.pallas_call(
        place_kernel,
        out_shape=(
            jax.ShapeDtypeStruct((group_rows, ff), BF16),
            jax.ShapeDtypeStruct((own, width), BF16),
            jax.ShapeDtypeStruct((2, slots, rows, blk), BF16),
        ),
        in_specs=[place] * 5,
        out_specs=(place, vmem, place),
        scratch_shapes=[
            pltpu.VMEM((blocks, own, LANES), F32),
            pltpu.VMEM((n_dp, n_t, packed, LANES), BF16),
            pltpu.VMEM((group_rows, ff), BF16),
            pltpu.VMEM((2, slots, rows, blk), BF16),
            pltpu.SMEM((n_t, hb, kmax), jnp.int32),
            pltpu.SMEM((1, slots), jnp.int32),
            dma((slots,)), dma((6,)),
        ],
        compiler_params=pltpu.CompilerParams(vmem_limit_bytes=60 * 1024 * 1024),
        name="place",
    )(cr, ca, block_home, hid, wg)


def solution(mesh):
    return jax.shard_map(
        functools.partial(body, mesh.shape["dp"], mesh.shape["tensor"]),
        mesh=mesh,
        in_specs=(
            P(("dp", "tensor"), None),
            P(None, "tensor", "dp", None),
            P("tensor", None),
            P("tensor"),
            P("tensor", None),
            P("dp", "tensor"),
        ),
        out_specs=(P("dp", "tensor"), P(("dp", "tensor"), None), P(None, "tensor", "dp", None)),
        check_vma=False,
    )
```
